256 devices in a mesh: dp: 4 (over y), tensor: 16 (over x_hi, z), rep: 4 (over x_lo, core).
Axes of the slice: x: 4 (x_hi: 2, x_lo: 2; x = x_hi * 2 + x_lo), y: 4, z: 8, core: 2. Of those that a mesh axis runs over, the one named last changes fastest.
Arguments:
- resid: bfloat16 [512, 8192], P('dp', 'rep'), may hold values from -94 to 94
- norm_gain: float32 [8192], P('rep'), may hold values from 0.25 to 1.75
- gate_weight: bfloat16 [4, 2048, 14336], P('rep', 'dp', 'tensor'), may hold values from -0.0625 to 0.0625
- up_weight: bfloat16 [4, 2048, 14336], P('rep', 'dp', 'tensor'), may hold values from -0.0625 to 0.0625
- down_weight: bfloat16 [14336, 4, 2048], P('tensor', 'rep', 'dp'), may hold values from -0.046875 to 0.046875
- enc_weight: bfloat16 [8192, 65536], P('rep', ('dp', 'tensor')), may hold values from -0.0625 to 0.0625
- enc_bias: float32 [65536], P(('dp', 'tensor')), may hold values from -3 to 3
- dec_weight: bfloat16 [65536, 8192], P(('dp', 'tensor'), 'rep'), may hold values from -1 to 1
- dec_bias: float32 [8192], P('rep'), may hold values from -3 to 3
- latent_ids: int32 [512, 64], replicated, may hold values from 0 to 65535, as said below
Outputs:
- resid_out: bfloat16 [512, 8192], P(('dp', 'tensor'), 'rep')
- recon: bfloat16 [512, 8192], P(('dp', 'tensor'), 'rep')
- error_ratio: float32 [512], P(('dp', 'tensor'))
The draws below stay inside these ranges and needn't reach their ends.
Inputs may be any that keep to these rules, and one draw needn't show every extreme that they name: `latent_ids`: each row names 64 distinct latents: 8 latents in each of 8 distinct blocks of 128 consecutive latents (block b holds latents b * 128 to b * 128 + 127).
All inputs are finite; a program needn't handle non-finite values.
Results may differ from the reference program's by a relative error of at most 0.009.
Values may be sent and summed in bfloat16 or wider, within the bound.
No kernel may reach another device: no remote copies, remote signals or barrier semaphores. Data moves between devices by JAX's collectives and lax.ppermute only.
A program may use at most 64 MiB of HBM per device.

```python
import math
from functools import partial
import jax
import jax.numpy as jnp
from jax import lax

D = 8192
FF = 14336
LAT = 65536
BLOCK = 128
NBLK_ACT = 8
PER_BLOCK = 8
ACTIVE = 64
TOKENS = 512
N_REP = 4


def draw_resid(key, part):
    key_rows, key_cols, key_base = jax.random.split(jax.random.fold_in(key, 7), 3)
    position = jnp.arange(D, dtype=jnp.float32) / D
    jitter = jax.random.uniform(key_cols, (1, D), jnp.float32, -0.4, 0.4)
    col_factor = jnp.exp(math.log(10.0) * (position[None, :] - 0.5) + jitter)
    spread_draw = jax.random.uniform(key_rows, (TOKENS, 1), jnp.float32)
    row_factor = jnp.exp(math.log(10.0) * (spread_draw - 0.5))
    base = jnp.clip(jax.random.normal(key_base, (TOKENS, D), jnp.float32), -5.0, 5.0)
    return (base * row_factor * col_factor).astype(jnp.bfloat16)


def draw_latent_ids(key, part):
    key_pop, key_noise, key_inner = jax.random.split(jax.random.fold_in(key, 11), 3)
    block_count = LAT // BLOCK
    popular = jax.random.randint(key_pop, (block_count,), 0, 512)
    noise = jax.random.randint(key_noise, (TOKENS, block_count), 0, 4096)
    scores = (noise + popular[None, :]) * block_count + jnp.arange(block_count, dtype=jnp.int32)[None, :]
    unused_a, blocks = lax.top_k(scores, NBLK_ACT)
    inner = jax.random.randint(key_inner, (TOKENS, NBLK_ACT, BLOCK), 0, 4096) * BLOCK + jnp.arange(BLOCK, dtype=jnp.int32)
    unused_b, picks = lax.top_k(inner, PER_BLOCK)
    chosen = blocks[:, :, None] * BLOCK + picks
    return chosen.reshape(TOKENS, NBLK_ACT * PER_BLOCK).astype(jnp.int32)


def level_of(stream_key, dims, shards, low, largest):
    gain = 1.0
    for dim, shards_of in shards:
        heights = jax.random.uniform(jax.random.fold_in(jax.random.fold_in(stream_key, 6), dim), (shards_of,), jnp.float32, low / len(shards), largest / len(shards))
        gain = gain * jnp.repeat(jnp.exp(heights), dims[dim] // shards_of).reshape((-1,) + (1,) * (len(dims) - 1 - dim))
    return gain


def normal_values(key, dims, spread, limit, cuts=(), kind=jnp.bfloat16):
    result = spread * jax.random.normal(key, dims, jnp.float32)
    if cuts:
        result = result * level_of(key, dims, cuts, -0.22, 0.18)
    return jnp.clip(result, -limit, limit).astype(kind)


def setup_inputs(seed: int = 0) -> dict:
    seeds = jax.random.split(jax.random.key(seed), 11)
    return {
        "resid": draw_resid(jax.random.fold_in(seeds[10], 71), 0),
        "norm_gain": jnp.clip(1.0 + 0.15 * jax.random.normal(seeds[1], (D,), jnp.float32), 0.25, 1.75),
        "gate_weight": normal_values(seeds[2], (N_REP, D // N_REP, FF), D ** -0.5, 0.0625, ((0, 4), (1, 4), (2, 16))),
        "up_weight": normal_values(seeds[3], (N_REP, D // N_REP, FF), D ** -0.5, 0.0625, ((0, 4), (1, 4), (2, 16))),
        "down_weight": normal_values(seeds[4], (FF, N_REP, D // N_REP), FF ** -0.5, 0.046875, ((0, 16), (1, 4), (2, 4))),
        "enc_weight": normal_values(seeds[5], (D, LAT), D ** -0.5, 0.0625, ((0, 4), (1, 64))),
        "enc_bias": normal_values(seeds[6], (LAT,), 0.5, 3.0, ((0, 64),), jnp.float32),
        "dec_weight": normal_values(seeds[7], (LAT, D), (ACTIVE // 2) ** -0.5, 1.0, ((0, 64), (1, 4))),
        "dec_bias": normal_values(seeds[8], (D,), 0.5, 3.0, ((0, 4),), jnp.float32),
        "latent_ids": draw_latent_ids(jax.random.fold_in(seeds[10], 71), 0),
    }


def decode_block(operands, enc_weight, enc_bias, dec_weight, dec_bias):
    centred, kept, latent_rows = operands
    columns = jnp.take(enc_weight, latent_rows, axis=1).astype(jnp.float32)
    preact = jnp.einsum('bd,dba->ba', centred.astype(jnp.float32), columns) + jnp.take(enc_bias, latent_rows)
    actives = jnp.maximum(preact, 0.0).astype(jnp.bfloat16)
    picked = jnp.take(dec_weight, latent_rows, axis=0).astype(jnp.float32)
    decoded = jnp.einsum('ba,bad->bd', actives.astype(jnp.float32), picked) + dec_bias[None, :]
    kept_f = kept.astype(jnp.float32)
    misfit = kept_f - decoded
    ratio = lax.optimization_barrier(jnp.sum(misfit * misfit, axis=1)) / (lax.optimization_barrier(jnp.sum(kept_f * kept_f, axis=1)) + 1e-06)
    return (decoded.astype(jnp.bfloat16), ratio)

def reference(resid, norm_gain, gate_weight, up_weight, down_weight, enc_weight, enc_bias, dec_weight, dec_bias, latent_ids):
    gate_full = gate_weight.reshape(D, FF)
    up_full = up_weight.reshape(D, FF)
    down_full = down_weight.reshape(FF, D)
    resid_f = resid.astype(jnp.float32)
    inverse_rms = lax.rsqrt(lax.optimization_barrier(jnp.mean(resid_f * resid_f, axis=1, keepdims=True)) + 1e-05)
    normed = (resid_f * inverse_rms * norm_gain[None, :]).astype(jnp.bfloat16)
    gate_pre = jnp.dot(normed, gate_full, preferred_element_type=jnp.float32)
    up_pre = jnp.dot(normed, up_full, preferred_element_type=jnp.float32)
    hidden = (jax.nn.silu(gate_pre) * up_pre).astype(jnp.bfloat16)
    block_sum = jnp.dot(hidden, down_full, preferred_element_type=jnp.float32)
    resid_out = (resid_f + block_sum).astype(jnp.bfloat16)
    centred = (resid_out.astype(jnp.float32) - dec_bias[None, :]).astype(jnp.bfloat16)
    count = TOKENS // 32
    operands = (centred.reshape(count, 32, D), resid_out.reshape(count, 32, D), latent_ids.reshape(count, 32, ACTIVE))
    decoded, ratio = lax.map(partial(decode_block, enc_weight=enc_weight, enc_bias=enc_bias, dec_weight=dec_weight, dec_bias=dec_bias), operands)
    return (resid_out, decoded.reshape(TOKENS, D), ratio.reshape(TOKENS))
```

```python
import jax
import jax.numpy as jnp
from jax import lax
from jax.experimental import pallas as pl
from jax.experimental.pallas import tpu as pltpu
from jax.sharding import Mesh, PartitionSpec as P

BF = jnp.bfloat16
F32 = jnp.float32
I32 = jnp.int32
VM = pl.BlockSpec(memory_space=pltpu.VMEM)
SM = pl.BlockSpec(memory_space=pltpu.SMEM)
MIB = 1 << 20


def call(kernel, outs, n_in, scratch, flops, nbytes, limit=32):
    return pl.pallas_call(
        kernel,
        out_shape=outs,
        in_specs=[SM] + [VM] * n_in,
        out_specs=jax.tree.map(lambda _: VM, outs),
        scratch_shapes=scratch,
        compiler_params=pltpu.CompilerParams(vmem_limit_bytes=limit * MIB),
        cost_estimate=pl.CostEstimate(flops=flops, bytes_accessed=nbytes, transcendentals=0),
    )


def sds(shape, dt):
    return jax.ShapeDtypeStruct(shape, dt)


def mm(a, b):
    return jnp.dot(a, b, preferred_element_type=F32)


def gate_up_kernel(pos, p0, p1, p2, p3, gain, go, gp, uo, up, *refs):
    outs, xsel, xg, pk, xr = refs[:8], refs[8], refs[9], refs[10], refs[11]
    for s, part in enumerate((p0, p1, p2, p3)):
        xr[s * 64:(s + 1) * 64, :] = part[...].astype(F32)
    xf = xr[...]
    xg[...] = (xf * gain[...]).astype(BF)
    ss = jnp.sum(xf * xf, axis=1, keepdims=True)
    hi = ss.astype(BF)
    lo = (ss - hi.astype(F32)).astype(BF)
    lane = lax.broadcasted_iota(I32, (256, 128), 1)
    tail = jnp.where(lane == 0, hi.astype(F32), jnp.where(lane == 1, lo.astype(F32), 0.0))
    pk[:, 1792:1920] = tail.astype(BF)
    a, b = xg[:, :512], xg[:, 512:]
    pk[:, :896] = (mm(a, go[...]) + mm(b, gp[...])).astype(BF)
    pk[:, 896:1792] = (mm(a, uo[...]) + mm(b, up[...])).astype(BF)
    for s in range(4):
        for e in range(2):
            half = pos[1] if e == 0 else 1 - pos[1]
            first = pl.multiple_of(((4 - s) % 4) * 64 + half * 32, 32)
            outs[s * 2 + e][...] = pk[pl.ds(first, 32), :]
    group = pos[4] // 2
    first = pl.multiple_of(lax.rem(pos[0] - group + 4, 4) * 64 + lax.rem(pos[4], 2) * 32, 32)
    col = pl.multiple_of(pos[3] * 256, 256)
    xsel[:, :256] = xr[pl.ds(first, 32), pl.ds(col, 256)]
    xsel[:, 256:] = xr[pl.ds(first, 32), pl.ds(512 + col, 256)]


def down_kernel(pos, *refs):
    parts, down_own, down_oth, out, hid = refs[:8], refs[8], refs[9], refs[10], refs[11]
    for s in range(4):
        for e in range(2):
            half = pos[1] if e == 0 else 1 - pos[1]
            first = pl.multiple_of(lax.rem(pos[0] - s + 4, 4) * 64 + half * 32, 32)
            hid[pl.ds(first, 32), :] = parts[s * 2 + e][...]
    for q, w in enumerate((down_own, down_oth)):
        y = mm(hid[...], w[...]).astype(BF)
        out[0, :, q * 256:(q + 1) * 256] = y[:, :256]
        out[1, :, q * 256:(q + 1) * 256] = y[:, 256:]


def table_kernel(pos, sid, out):
    lane128 = lax.broadcasted_iota(I32, (32, 128), 1)

    def step(t, carry):
        rows = pl.ds(pl.multiple_of(t * 32, 32), 32)
        ids = sid[rows, :]
        base = jnp.where(t >= 8, 64, 0)
        slots = []
        for s in range(8):
            acc = jnp.full((32, 128), -1, I32)
            for i in range(8):
                j = s * 8 + i
                acc = jnp.where((ids[:, j:j + 1] & 127) == lane128, base + j, acc)
            slots.append((ids[:, s * 8:s * 8 + 1] >> 7, acc))
        for k in range(2):
            block0 = pos[5 + k] >> 7
            for b in range(8):
                acc = jnp.full((32, 128), -1, I32)
                for block, slot in slots:
                    acc = jnp.where(block == block0 + b, slot, acc)
                out[rows, (k * 8 + b) * 128:(k * 8 + b + 1) * 128] = acc
        return carry

    lax.fori_loop(0, 16, step, 0)


def lookup(values, index):
    return jnp.take_along_axis(values, index, axis=1, mode="promise_in_bounds")


def encode_kernel(pos, p0, p1, p2, p3, enc, encp, bias, dec_bias, sidp, out, pre):
    lane128 = lax.broadcasted_iota(I32, (64, 128), 1)
    cent = []
    for s, part in enumerate((p0, p1, p2, p3)):
        g = lax.rem(pos[0] - s + 4, 4)
        col = pl.multiple_of(g * 512 + pos[3] * 256, 256)
        cent.append((part[...].astype(F32) - dec_bias[:, pl.ds(col, 256)]).astype(BF))
    for k in range(2):
        acc = None
        for s in range(4):
            g = lax.rem(pos[0] - s + 4, 4)
            if k == 0:
                w = enc[pl.ds(pl.multiple_of(g * 512 + pos[3] * 256, 256), 256), :]
            else:
                w = encp[pl.ds(pl.multiple_of(g * 256, 256), 256), :]
            term = mm(cent[s], w)
            acc = term if acc is None else acc + term
        if k == 0:
            acc = acc + bias[...]
        pre[k, :, :] = acc
    for t in range(4):
        ids = sidp[t * 64:(t + 1) * 64, :]
        lane = ids & 127
        acc = jnp.zeros((64, 128), F32)
        for k in range(2):
            block = (ids >> 7) - (pos[5 + k] >> 7)
            for b in range(8):
                lo = lookup(pre[k, t * 64:(t + 1) * 64, b * 128:(b + 1) * 128], lane)
                hi = lookup(pre[k, 256 + t * 64:256 + (t + 1) * 64, b * 128:(b + 1) * 128], lane)
                acc = jnp.where(block == b, jnp.where(lane128 < 64, lo, hi), acc)
        out[t * 64:(t + 1) * 64, :] = acc.astype(BF)


def decode_kernel(pos, *refs):
    parts, table, dec, decp = refs[:8], refs[8], refs[9], refs[10]
    outs, act, dense, y = refs[11:15], refs[15], refs[16], refs[17]
    total = parts[0][...].astype(F32)
    for part in parts[1:]:
        total = total + part[...].astype(F32)
    act[...] = jnp.maximum(total, 0.0)

    def step(t, carry):
        rows = pl.ds(pl.multiple_of(t * 64, 64), 64)
        vals = act[pl.ds(pl.multiple_of(lax.rem(t, 4) * 64, 64), 64), :]
        for b in range(16):
            idx = table[rows, b * 128:(b + 1) * 128]
            got = lookup(vals, jnp.maximum(idx, 0))
            dense[rows, b * 128:(b + 1) * 128] = jnp.where(idx >= 0, got, 0.0).astype(BF)
        return carry

    lax.fori_loop(0, 8, step, 0)
    for g in range(4):
        col = pl.multiple_of(g * 512 + pos[3] * 256, 256)
        r = mm(dense[:, :1024], dec[:, pl.ds(col, 256)])
        r = r + mm(dense[:, 1024:], decp[:, g * 256:(g + 1) * 256])
        y[:, g * 256:(g + 1) * 256] = r.astype(BF)
    for s in range(4):
        first = pl.multiple_of(lax.rem(pos[0] + s, 4) * 128, 128)
        outs[s][...] = y[pl.ds(first, 128), :]


def shift(x, axes, sizes, offset, flip):
    total = 1
    for n in sizes:
        total *= n
    pairs = []
    for i in range(total):
        rest, coords = i, []
        for n in reversed(sizes):
            coords.append(rest % n)
            rest //= n
        coords = coords[::-1]
        j = 0
        for cc, n, o, f in zip(coords, sizes, offset, flip):
            j = j * n + (cc ^ o if f else (cc + o) % n)
        pairs.append((i, j))
    return lax.ppermute(x, axes, pairs)


def swap(x, axis):
    return lax.ppermute(x, axis, [(0, 1), (1, 0)])


def dp_shift(x, s):
    return lax.ppermute(x, "dp", [(i, (i + s) % 4) for i in range(4)])


def dpx_shift(x, s, e):
    return shift(x, ("dp", "xlo"), (4, 2), (s, e), (False, True))


def body(resid, norm_gain, gate_w, up_w, down_w, enc, enc_bias, dec, dec_bias, ids):
    d, x, c = lax.axis_index("dp"), lax.axis_index("xlo"), lax.axis_index("core")
    h, z = lax.axis_index("xhi"), lax.axis_index("z")
    slab = ((d * 2 + h) * 8 + z) * 1024
    slab_p = ((d * 2 + 1 - h) * 8 + z) * 1024
    pos = jnp.stack([d, x, c, h, z, slab, slab_p, slab]).astype(I32)

    x4 = resid.reshape(4, 2, 16, 2048)
    mine = lax.dynamic_index_in_dim(x4, c, 1, keepdims=False).reshape(64, 2048)
    give = lax.dynamic_index_in_dim(x4, 1 - c, 1, keepdims=False).reshape(64, 2048)
    other = swap(give, "core")
    gain_o = swap(norm_gain.reshape(1, 2048), "core")
    gate, up, down = gate_w[0], up_w[0], down_w[:, 0, :]
    gate_o, up_o = swap(gate, "core"), swap(up, "core")

    def width_slice(g):
        return jnp.concatenate(
            [lax.dynamic_slice_in_dim(a, g * 512, 512, 1) for a in (mine, other)], axis=1
        )

    xs = [width_slice(d)] + [dp_shift(width_slice((d + s) % 4), s) for s in range(1, 4)]
    down_o = swap(down, "core")
    encp = swap(
        lax.dynamic_index_in_dim(enc.reshape(4, 2, 256, 1024), 1 - h, 1, keepdims=False).reshape(1024, 1024),
        "xhi",
    )
    decp = swap(
        lax.dynamic_index_in_dim(dec.reshape(1024, 4, 2, 256), 1 - h, 2, keepdims=False).reshape(1024, 1024),
        "xhi",
    )
    gain = jnp.concatenate(
        [lax.dynamic_slice_in_dim(a, d * 512, 512, 1) for a in (norm_gain.reshape(1, 2048), gain_o)], axis=1
    )

    rank = jnp.sum((ids[:, :, None] < ids[:, None, :]).astype(I32), axis=1)
    place = lax.broadcasted_iota(I32, (1, 64, 64), 1)
    sid = jnp.sum(jnp.where(rank[:, None, :] == place, ids[:, None, :], 0), axis=2)
    sidp = jnp.concatenate([sid[:256], sid[256:]], axis=1)
    table = call(table_kernel, sds((512, 2048), I32), 1, [], 200_000_000, 5_000_000)(pos, sid)

    outs = [sds((32, 1920), BF)] * 8 + [sds((32, 512), F32)]
    res = call(
        gate_up_kernel, outs, 9,
        [pltpu.VMEM((256, 1024), BF), pltpu.VMEM((256, 1920), BF), pltpu.VMEM((256, 1024), F32)],
        940_000_000, 6_000_000,
    )(pos, *xs, gain, gate, gate_o, up, up_o)
    xsel = res[8]
    got = [res[0]] + [dpx_shift(res[s * 2 + e], s, e) for s in range(4) for e in range(2) if s + e]
    tot = got[0].astype(F32)
    for p in got[1:]:
        tot = tot + p.astype(F32)
    inv = lax.rsqrt((tot[:, 1792:1793] + tot[:, 1793:1794]) / 8192 + 1e-05)
    hidden = (jax.nn.silu(tot[:, :896] * inv) * (tot[:, 896:1792] * inv)).astype(BF)
    hid = [hidden] + [dpx_shift(hidden, s, e) for s in range(4) for e in range(2) if s + e]
    terms = call(
        down_kernel, sds((2, 256, 512), BF), 10, [pltpu.VMEM((256, 896), BF)], 470_000_000, 3_000_000
    )(pos, *hid, down, down_o)
    terms = lax.all_to_all(terms.reshape(512, 512), ("xhi", "z"), 0, 0, tiled=True)
    block_sum = jnp.sum(terms.reshape(16, 32, 512).astype(F32), axis=0)
    rows = (xsel + block_sum).astype(BF)

    own, crossed = rows[:, :256].reshape(2, 16, 256), swap(rows[:, 256:], "core").reshape(2, 16, 256)
    rows = jnp.where(c == 0, jnp.stack([own, crossed], 1), jnp.stack([crossed, own], 1)).reshape(64, 256)
    rows = jnp.broadcast_to(rows[None], (8, 64, 256)).reshape(512, 256)
    rows = lax.all_to_all(rows, "z", 0, 0, tiled=True)
    parts = [rows] + [dp_shift(rows, s) for s in range(1, 4)]

    kept_rel = jnp.stack(
        [
            jnp.concatenate([lax.dynamic_slice_in_dim(p, d * 128 + b * 64 + z * 8, 8, 0) for b in range(2)], 0)
            for p in parts
        ]
    )
    kept = jnp.stack(
        [lax.dynamic_index_in_dim(kept_rel, (d - g + 4) % 4, 0, keepdims=False) for g in range(4)], 1
    )
    kept_peer = swap(lax.dynamic_slice_in_dim(kept, (1 - h) * 8, 8, 0), "xhi")

    lead = ((x == 0) & (c == 0)).astype(F32)
    comp = call(
        encode_kernel, sds((256, 128), BF), 9, [pltpu.VMEM((2, 512, 1024), F32)],
        2_200_000_000, 8_000_000,
    )(pos, *parts, enc, encp, (enc_bias * lead).reshape(1, 1024), dec_bias.reshape(1, 2048), sidp)
    comps = [comp] + [
        shift(comp, ("xhi", "xlo", "core"), (2, 2, 2), (o >> 2, (o >> 1) & 1, o & 1), (True, True, True))
        for o in range(1, 8)
    ]
    ys = call(
        decode_kernel, [sds((128, 1024), BF)] * 4, 11,
        [pltpu.VMEM((256, 128), F32), pltpu.VMEM((512, 2048), BF), pltpu.VMEM((512, 1024), BF)],
        2_200_000_000, 12_000_000,
    )(pos, *comps, table, dec, decp)
    y = ys[0].astype(F32)
    for s in range(1, 4):
        y = y + dp_shift(ys[s], s).astype(F32)
    y = y.astype(BF).reshape(2, 8, 8, 1024).transpose(1, 0, 2, 3).reshape(128, 1024)
    y = lax.all_to_all(y, "z", 0, 0, tiled=True)
    bias_h = lax.dynamic_index_in_dim(dec_bias.reshape(4, 2, 256), h, 1, keepdims=False)
    decoded = jnp.sum(y.reshape(8, 16, 4, 256).astype(F32), axis=0) + bias_h[None]
    recon = decoded.astype(BF)
    recon_peer = swap(lax.dynamic_slice_in_dim(recon, (1 - h) * 8, 8, 0), "xhi")
    kept_f = kept.astype(F32)
    misfit = kept_f - decoded
    sums = jnp.concatenate([jnp.sum(misfit * misfit, axis=(1, 2)), jnp.sum(kept_f * kept_f, axis=(1, 2))])
    sums = lax.psum(sums, ("xhi", "xlo", "core")).reshape(2, 2, 8)
    sums = lax.dynamic_index_in_dim(sums, h, 1, keepdims=False)
    ratio = sums[0] / (sums[1] + 1e-06)

    def join(mine16, peer8):
        own8 = lax.dynamic_slice_in_dim(mine16, h * 8, 8, 0)
        both = jnp.where(h == 0, jnp.stack([own8, peer8], 2), jnp.stack([peer8, own8], 2))
        return both.reshape(8, 2048)

    return join(kept, kept_peer), join(recon, recon_peer), ratio


def solution(mesh):
    fine = Mesh(mesh.devices.reshape(4, 2, 8, 2, 2), ("dp", "xhi", "z", "xlo", "core"))
    rep, tensor, slabs = ("xlo", "core"), ("xhi", "z"), ("dp", "xhi", "z")
    in_specs = (
        P("dp", rep), P(rep), P(rep, "dp", tensor), P(rep, "dp", tensor), P(tensor, rep, "dp"),
        P(rep, slabs), P(slabs), P(slabs, rep), P(rep), P(),
    )
    out_specs = (P(slabs, rep), P(slabs, rep), P(slabs))
    return jax.shard_map(body, mesh=fine, in_specs=in_specs, out_specs=out_specs, check_vma=False)
```

```python
import jax
import jax.numpy as jnp
from jax import lax
from jax.experimental import pallas as pl
from jax.experimental.pallas import tpu as pltpu
from jax.sharding import Mesh, PartitionSpec as P

BF = jnp.bfloat16
F32 = jnp.float32
I32 = jnp.int32
VM = pl.BlockSpec(memory_space=pltpu.VMEM)
SM = pl.BlockSpec(memory_space=pltpu.SMEM)
ANY = pl.BlockSpec(memory_space=pltpu.HBM)
MIB = 1 << 20


def call(kernel, outs, n_in, scratch, flops, nbytes, limit=12, any_at=(), any_out=False):
    in_specs = [SM] + [ANY if i in any_at else VM for i in range(n_in)]
    return pl.pallas_call(
        kernel,
        out_shape=outs,
        in_specs=in_specs,
        out_specs=jax.tree.map(lambda _: ANY if any_out else VM, outs),
        scratch_shapes=scratch,
        compiler_params=pltpu.CompilerParams(vmem_limit_bytes=limit * MIB),
        cost_estimate=pl.CostEstimate(flops=flops, bytes_accessed=nbytes, transcendentals=0),
    )


def sds(shape, dt):
    return jax.ShapeDtypeStruct(shape, dt)


def mm(a, b):
    return jnp.dot(a, b, preferred_element_type=F32)


NC = 2
ROWS = 512 // NC
PER = 128 // NC


def gate_kernel(pos, p0, p1, p2, p3, gain, go, gp, *refs):
    outs, xsel, xg, pk, xr = refs[:4], refs[4], refs[5], refs[6], refs[7]
    for s, part in enumerate((p0, p1, p2, p3)):
        xr[s * 64:(s + 1) * 64, :] = part[...].astype(F32)
    xf = xr[...]
    xg[...] = (xf * gain[...]).astype(BF)
    ss = jnp.sum(xf * xf, axis=1, keepdims=True)
    hi = ss.astype(BF)
    lo = (ss - hi.astype(F32)).astype(BF)
    lane = lax.broadcasted_iota(I32, (256, 128), 1)
    tail = jnp.where(lane == 0, hi.astype(F32), jnp.where(lane == 1, lo.astype(F32), 0.0))
    pk[:, 896:] = tail.astype(BF)
    pk[:, :896] = (mm(xg[:, :512], go[...]) + mm(xg[:, 512:], gp[...])).astype(BF)
    for s in range(4):
        first = ((4 - s) % 4) * 64
        outs[s][...] = pk[first:first + 64, :]
    group = pos[3] // 4
    first = pl.multiple_of(lax.rem(pos[0] - group + 4, 4) * 64 + lax.rem(pos[3], 4) * 16, 16)
    xsel[...] = xr[pl.ds(first, 16), :]


def up_kernel(pos, xg, uo, up, *refs):
    outs, pk = refs[:4], refs[4]
    pk[...] = (mm(xg[:, :512], uo[...]) + mm(xg[:, 512:], up[...])).astype(BF)
    for s in range(4):
        first = ((4 - s) % 4) * 64
        outs[s][...] = pk[first:first + 64, :]


def down_kernel(pos, *refs):
    parts, down_own, down_oth, out, hid = refs[:4], refs[4], refs[5], refs[6], refs[7]
    for s in range(4):
        first = pl.multiple_of(lax.rem(pos[0] - s + 4, 4) * 64, 64)
        hid[pl.ds(first, 64), :] = parts[s][...]
    for q, w in enumerate((down_own, down_oth)):
        out[:, q * 512:(q + 1) * 512] = mm(hid[...], w[...]).astype(BF)


def split_kernel(pos, resid, mine, give):
    c = pos[2]
    for b in range(4):
        mine[b * 16:(b + 1) * 16, :] = resid[pl.ds(pl.multiple_of(b * 32 + c * 16, 16), 16), :]
        give[b * 16:(b + 1) * 16, :] = resid[pl.ds(pl.multiple_of(b * 32 + (1 - c) * 16, 16), 16), :]


def width_kernel(pos, mine, other, gain, gain_o, *outs):
    for s in range(4):
        col = pl.multiple_of(lax.rem(pos[0] + s, 4) * 512, 512)
        outs[s][:, :512] = mine[:, pl.ds(col, 512)]
        outs[s][:, 512:] = other[:, pl.ds(col, 512)]
    col = pl.multiple_of(pos[0] * 512, 512)
    outs[4][:, :512] = gain[:, pl.ds(col, 512)]
    outs[4][:, 512:] = gain_o[:, pl.ds(col, 512)]


def table_kernel(pos, sid, out):
    lane128 = lax.broadcasted_iota(I32, (32, 128), 1)
    block0 = pos[4] >> 7

    def step(t, carry):
        rows = pl.ds(pl.multiple_of(t * 32, 32), 32)
        ids = sid[rows, :]
        base = jnp.where(lax.rem(t, ROWS // 32) >= ROWS // 64, 64, 0)
        slots = []
        for s in range(8):
            acc = jnp.full((32, 128), -1, I32)
            for i in range(8):
                j = s * 8 + i
                acc = jnp.where((ids[:, j:j + 1] & 127) == lane128, base + j, acc)
            slots.append((jnp.broadcast_to((ids[:, s * 8:s * 8 + 1] >> 7) - block0, (32, 128)), acc))
        for b in range(8):
            acc = jnp.full((32, 128), -1, I32)
            for block, slot in slots:
                acc = jnp.where(block == b, slot, acc)
            out[rows, b * 128:(b + 1) * 128] = acc.astype(jnp.int8)
        return carry

    lax.fori_loop(0, 16, step, 0)


def lookup(values, index):
    return jnp.take_along_axis(values, index, axis=1, mode="promise_in_bounds")


def encode_kernel(pos, p0, p1, p2, p3, enc, bias, dec_bias, sidp, out, cent, pre):
    lane128 = lax.broadcasted_iota(I32, (64, 128), 1)
    for s, part in enumerate((p0, p1, p2, p3)):
        at = pl.ds(pl.multiple_of(lax.rem(pos[0] - s + 4, 4) * 512, 512), 512)
        cent[:, at] = (part[...].astype(F32) - dec_bias[:, at]).astype(BF)

    def product(n, carry):
        cols = pl.ds(pl.multiple_of(n * 256, 256), 256)
        pre[:, cols] = mm(cent[...], enc[:, cols]) + bias[:, cols]
        return carry

    lax.fori_loop(0, 4, product, 0)

    def compress(t, carry):
        rows = pl.ds(pl.multiple_of(t * 64, 64), 64)
        rows_hi = pl.ds(pl.multiple_of(ROWS // 2 + t * 64, 64), 64)
        ids = sidp[rows, :]
        lane = ids & 127
        block = (ids >> 7) - (pos[4] >> 7)
        acc = jnp.zeros((64, 128), F32)
        for b in range(8):
            lo = lookup(pre[rows, b * 128:(b + 1) * 128], lane)
            hi = lookup(pre[rows_hi, b * 128:(b + 1) * 128], lane)
            acc = jnp.where(block == b, jnp.where(lane128 < 64, lo, hi), acc)
        out[rows, :] = acc
        return carry

    lax.fori_loop(0, ROWS // 128, compress, 0)


def decode_kernel(pos, total, table, dec, *refs):
    outs, act, dense, y = refs[:4], refs[4], refs[5], refs[6]
    act[...] = jnp.maximum(total[...], 0.0)

    def step(t, carry):
        rows = pl.ds(pl.multiple_of(t * 64, 64), 64)
        vals = act[pl.ds(pl.multiple_of(lax.rem(t, ROWS // 128) * 64, 64), 64), :]
        for b in range(8):
            idx = table[rows, b * 128:(b + 1) * 128].astype(I32)
            got = lookup(vals, jnp.maximum(idx, 0))
            dense[rows, b * 128:(b + 1) * 128] = jnp.where(idx >= 0, got, 0.0).astype(BF)
        return carry

    lax.fori_loop(0, ROWS // 64, step, 0)

    def product(g, carry):
        at = pl.ds(pl.multiple_of(g * 256, 256), 256)
        y[:, at] = mm(dense[...], dec[:, at]).astype(BF)
        return carry

    lax.fori_loop(0, 8, product, 0)
    for s in range(4):
        first = pl.multiple_of(lax.rem(pos[0] + s, 4) * PER, PER)
        outs[s][...] = y[pl.ds(first, PER), :]


def swap(x, axis):
    return lax.ppermute(x, axis, [(0, 1), (1, 0)])


def dp_shift(x, s):
    return lax.ppermute(x, "dp", [(i, (i + s) % 4) for i in range(4)])


def body(resid, norm_gain, gate_w, up_w, down_w, enc, enc_bias, dec, dec_bias, ids):
    d, x, c = lax.axis_index("dp"), lax.axis_index("xlo"), lax.axis_index("core")
    h, z = lax.axis_index("xhi"), lax.axis_index("z")
    tensor = h * 8 + z
    pos = jnp.stack([d, x, c, tensor, (d * 16 + tensor) * 1024, d, d, d]).astype(I32)

    wide = norm_gain.reshape(1, 2048)
    mine, give = call(split_kernel, [sds((64, 2048), BF)] * 2, 1, [], 0, 1_000_000)(pos, resid)
    other, gain_o = swap(give, "core"), swap(wide, "core")
    gate, up, down = gate_w[0], up_w[0], down_w[:, 0, :]
    gate_o, up_o, down_o = swap(gate, "core"), swap(up, "core"), swap(down, "core")
    *xw, gain = call(
        width_kernel, [sds((64, 1024), BF)] * 4 + [sds((1, 1024), F32)], 4, [], 0, 1_000_000
    )(pos, mine, other, wide, gain_o)
    xs = [xw[0]] + [dp_shift(xw[s], s) for s in range(1, 4)]

    rank = jnp.sum((ids[:, :, None] < ids[:, None, :]).astype(I32), axis=1)
    place = lax.broadcasted_iota(I32, (1, 64, 64), 1)
    sid = jnp.sum(jnp.where(rank[:, None, :] == place, ids[:, None, :], 0), axis=2)
    sid = sid.reshape(4, NC, PER, 64).transpose(1, 0, 2, 3)
    sidp = sid.reshape(NC, 2, ROWS // 2, 64).transpose(0, 2, 1, 3).reshape(NC, ROWS // 2, 128)

    res = call(
        gate_kernel, [sds((64, 1024), BF)] * 4 + [sds((16, 1024), F32), sds((256, 1024), BF)], 7,
        [pltpu.VMEM((256, 1024), BF), pltpu.VMEM((256, 1024), F32)], 470_000_000, 3_000_000,
    )(pos, *xs, gain, gate, gate_o)
    xsel, xg = res[4], res[5]
    res_u = call(
        up_kernel, [sds((64, 896), BF)] * 4, 3, [pltpu.VMEM((256, 896), BF)], 470_000_000, 3_000_000
    )(pos, xg, up, up_o)

    def width_sum(pieces):
        tot = pieces[0].astype(F32)
        for s in range(1, 4):
            tot = tot + dp_shift(pieces[s], s).astype(F32)
        return tot + swap(tot.astype(BF), "xlo").astype(F32)

    tot_g, tot_u = width_sum(res[:4]), width_sum(res_u)
    inv = lax.rsqrt((tot_g[:, 896:897] + tot_g[:, 897:898]) / 8192 + 1e-05)
    hidden = (jax.nn.silu(tot_g[:, :896] * inv) * (tot_u * inv)).astype(BF)
    hid = [hidden] + [dp_shift(hidden, s) for s in range(1, 4)]
    terms = call(
        down_kernel, sds((256, 1024), BF), 6, [pltpu.VMEM((256, 896), BF)], 470_000_000, 3_000_000
    )(pos, *hid, down, down_o)
    terms = lax.all_to_all(terms, ("xhi", "z"), 0, 0, tiled=True)
    block_sum = jnp.sum(terms.reshape(16, 16, 1024).astype(F32), axis=0)
    rows = (xsel + block_sum).astype(BF)

    own, crossed = rows[:, :512], swap(rows[:, 512:], "core")
    rows = jnp.where(c == 0, jnp.stack([own, crossed]), jnp.stack([crossed, own])).reshape(32, 512)
    rows = jnp.broadcast_to(rows[None], (16, 32, 512)).reshape(512, 512)
    rows = lax.all_to_all(rows, ("xhi", "z"), 0, 0, tiled=True)
    rows = rows.reshape(4, NC, PER, 512)
    parts = []
    for k in range(NC):
        chunk = rows[:, k].reshape(ROWS, 512)
        if k:
            chunk, _ = lax.optimization_barrier((chunk, parts[-1]))
        parts.append([chunk] + [dp_shift(chunk, s) for s in range(1, 4)])

    at, _ = lax.optimization_barrier((pos, rows))
    table = call(table_kernel, sds((512, 1024), jnp.int8), 1, [], 1_000_000_000, 20_000_000)(
        at, sid.reshape(512, 64)
    )
    sidp, table = lax.optimization_barrier((sidp, table))

    chunk_of = tensor * 8 // PER
    first = d * PER + lax.rem(tensor * 8, PER)
    picks = [
        jnp.stack([lax.dynamic_slice_in_dim(p, first, 8, 0) for p in parts[k]]) for k in range(NC)
    ]
    rel = picks[0]
    for k in range(1, NC):
        rel = jnp.where(chunk_of == k, picks[k], rel)
    kept = jnp.concatenate(
        [lax.dynamic_index_in_dim(rel, (d - g + 4) % 4, 0, keepdims=False) for g in range(4)], 1
    )

    lead = ((x == 0) & (c == 0)).astype(F32)
    bias = (enc_bias * lead).reshape(1, 1024)
    wide_bias = dec_bias.reshape(1, 2048)
    pieces = []
    for k in range(NC):
        comp = call(
            encode_kernel, sds((ROWS // 2, 128), F32), 8,
            [pltpu.VMEM((ROWS, 2048), BF), pltpu.VMEM((ROWS, 1024), F32)],
            2_200_000_000 // NC, 6_000_000, limit=20,
        )(pos, *parts[k], enc, bias, wide_bias, sidp[k])
        for axis in ("core", "xlo"):
            comp = comp + swap(comp.astype(BF), axis).astype(F32)
        ys = call(
            decode_kernel, [sds((PER, 2048), BF)] * 4, 3,
            [pltpu.VMEM((ROWS // 2, 128), F32), pltpu.VMEM((ROWS, 1024), BF), pltpu.VMEM((ROWS, 2048), BF)],
            2_200_000_000 // NC, 8_000_000, limit=20,
        )(pos, comp, table[k * ROWS:(k + 1) * ROWS], dec)
        y = ys[0].astype(F32)
        for s in range(1, 4):
            y = y + dp_shift(ys[s], s).astype(F32)
        pieces.append(y.astype(BF))
    y = lax.all_to_all(jnp.concatenate(pieces, 0), ("xhi", "z"), 0, 0, tiled=True)
    decoded = jnp.sum(y.reshape(16, 8, 2048).astype(F32), axis=0) + wide_bias
    kept_f = kept.astype(F32)
    misfit = kept_f - decoded
    sums = jnp.stack([jnp.sum(misfit * misfit, axis=1), jnp.sum(kept_f * kept_f, axis=1)])
    for axis in ("core", "xlo"):
        sums = sums + swap(sums, axis)
    return kept, decoded.astype(BF), sums[0] / (sums[1] + 1e-06)


def solution(mesh):
    fine = Mesh(mesh.devices.reshape(4, 2, 8, 2, 2), ("dp", "xhi", "z", "xlo", "core"))
    rep, tensor, slabs = ("xlo", "core"), ("xhi", "z"), ("dp", "xhi", "z")
    in_specs = (
        P("dp", rep), P(rep), P(rep, "dp", tensor), P(rep, "dp", tensor), P(tensor, rep, "dp"),
        P(rep, slabs), P(slabs), P(slabs, rep), P(rep), P(),
    )
    out_specs = (P(slabs, rep), P(slabs, rep), P(slabs))
    return jax.shard_map(body, mesh=fine, in_specs=in_specs, out_specs=out_specs, check_vma=False)
```

```python
import jax
import jax.numpy as jnp
from jax import lax
from jax.experimental import pallas as pl
from jax.experimental.pallas import tpu as pltpu
from jax.sharding import Mesh, PartitionSpec as P

BF = jnp.bfloat16
F32 = jnp.float32
I32 = jnp.int32
VM = pl.BlockSpec(memory_space=pltpu.VMEM)
SM = pl.BlockSpec(memory_space=pltpu.SMEM)
ANY = pl.BlockSpec(memory_space=pltpu.HBM)
MIB = 1 << 20


def call(kernel, outs, n_in, scratch, flops, nbytes, limit=12, any_at=(), any_out=False):
    in_specs = [SM] + [ANY if i in any_at else VM for i in range(n_in)]
    return pl.pallas_call(
        kernel,
        out_shape=outs,
        in_specs=in_specs,
        out_specs=jax.tree.map(lambda _: ANY if any_out else VM, outs),
        scratch_shapes=scratch,
        compiler_params=pltpu.CompilerParams(vmem_limit_bytes=limit * MIB),
        cost_estimate=pl.CostEstimate(flops=flops, bytes_accessed=nbytes, transcendentals=0),
    )


def sds(shape, dt):
    return jax.ShapeDtypeStruct(shape, dt)


def mm(a, b):
    return jnp.dot(a, b, preferred_element_type=F32)


SEATS = 64
ROWS = 4 * SEATS


def gate_kernel(pos, p0, p1, p2, p3, gain, go, gp, *refs):
    outs, xsel, xg, pk, xr = refs[:4], refs[4], refs[5], refs[6], refs[7]
    for s, part in enumerate((p0, p1, p2, p3)):
        xr[s * 64:(s + 1) * 64, :] = part[...].astype(F32)
    xf = xr[...]
    xg[...] = (xf * gain[...]).astype(BF)
    ss = jnp.sum(xf * xf, axis=1, keepdims=True)
    hi = ss.astype(BF)
    lo = (ss - hi.astype(F32)).astype(BF)
    lane = lax.broadcasted_iota(I32, (256, 128), 1)
    tail = jnp.where(lane == 0, hi.astype(F32), jnp.where(lane == 1, lo.astype(F32), 0.0))
    pk[:, 896:] = tail.astype(BF)
    pk[:, :896] = (mm(xg[:, :512], go[...]) + mm(xg[:, 512:], gp[...])).astype(BF)
    for s in range(4):
        first = ((4 - s) % 4) * 64
        outs[s][...] = pk[first:first + 64, :]
    group = pos[3] // 4
    first = pl.multiple_of(lax.rem(pos[0] - group + 4, 4) * 64 + lax.rem(pos[3], 4) * 16, 16)
    xsel[...] = xr[pl.ds(first, 16), :]


def up_kernel(pos, xg, uo, up, *refs):
    outs, pk = refs[:4], refs[4]
    pk[...] = (mm(xg[:, :512], uo[...]) + mm(xg[:, 512:], up[...])).astype(BF)
    for s in range(4):
        first = ((4 - s) % 4) * 64
        outs[s][...] = pk[first:first + 64, :]


def down_kernel(pos, *refs):
    parts, down_own, down_oth, out, hid = refs[:4], refs[4], refs[5], refs[6], refs[7]
    for s in range(4):
        first = pl.multiple_of(lax.rem(pos[0] - s + 4, 4) * 64, 64)
        hid[pl.ds(first, 64), :] = parts[s][...]
    for q, w in enumerate((down_own, down_oth)):
        out[:, q * 512:(q + 1) * 512] = mm(hid[...], w[...]).astype(BF)


def split_kernel(pos, resid, mine, give):
    c = pos[2]
    for b in range(4):
        mine[b * 16:(b + 1) * 16, :] = resid[pl.ds(pl.multiple_of(b * 32 + c * 16, 16), 16), :]
        give[b * 16:(b + 1) * 16, :] = resid[pl.ds(pl.multiple_of(b * 32 + (1 - c) * 16, 16), 16), :]


def width_kernel(pos, mine, other, gain, gain_o, *outs):
    for s in range(4):
        col = pl.multiple_of(lax.rem(pos[0] + s, 4) * 512, 512)
        outs[s][:, :512] = mine[:, pl.ds(col, 512)]
        outs[s][:, 512:] = other[:, pl.ds(col, 512)]
    col = pl.multiple_of(pos[0] * 512, 512)
    outs[4][:, :512] = gain[:, pl.ds(col, 512)]
    outs[4][:, 512:] = gain_o[:, pl.ds(col, 512)]


def table_kernel(pos, sid, out):
    lane128 = lax.broadcasted_iota(I32, (32, 128), 1)
    block0 = pos[4] >> 7

    def step(t, carry):
        rows = pl.ds(pl.multiple_of(t * 32, 32), 32)
        ids = sid[rows, :]
        base = jnp.where(t >= ROWS // 64, 64, 0)
        slots = []
        for s in range(8):
            acc = jnp.full((32, 128), -1, I32)
            for i in range(8):
                j = s * 8 + i
                acc = jnp.where((ids[:, j:j + 1] & 127) == lane128, base + j, acc)
            slots.append((jnp.broadcast_to((ids[:, s * 8:s * 8 + 1] >> 7) - block0, (32, 128)), acc))
        for b in range(8):
            acc = jnp.full((32, 128), -1, I32)
            for block, slot in slots:
                acc = jnp.where(block == b, slot, acc)
            out[rows, b * 128:(b + 1) * 128] = acc.astype(jnp.int8)
        return carry

    lax.fori_loop(0, ROWS // 32, step, 0)


def chosen(rank, row, start):
    seat = lax.broadcasted_iota(I32, (SEATS, 128), 0)
    return jnp.where(rank[pl.ds(row, 1), :] == seat + start, 1.0, 0.0).astype(BF)


def pack_kernel(start):
    def kernel(pos, rows, rank, *outs):
        for s in range(4):
            slab = lax.rem(pos[0] + s, 4)
            for g in range(4):
                pick = chosen(rank, slab * 4 + g, start)
                outs[s][g * SEATS:(g + 1) * SEATS, :] = mm(pick, rows[g * 128:(g + 1) * 128, :]).astype(BF)

    return kernel


def ids_kernel(start):
    def kernel(pos, hi, lo, rank, out):
        for g in range(4):
            pick = chosen(rank, pos[0] * 4 + g, start)
            at = slice(g * 128, (g + 1) * 128)
            both = mm(pick, hi[at, :]) * 256.0 + mm(pick, lo[at, :])
            out[g * SEATS:(g + 1) * SEATS, :] = both.astype(I32) - 1

    return kernel


def unpack_kernel(start):
    def kernel(pos, p0, p1, p2, p3, rank, out, picks, vals):
        for s, part in enumerate((p0, p1, p2, p3)):
            slab = lax.rem(pos[0] - s + 4, 4)
            picks[s * SEATS:(s + 1) * SEATS, :] = chosen(rank, slab * 4 + pos[0], start)
            vals[s * SEATS:(s + 1) * SEATS, :] = part[...]

        def product(n, carry):
            at = pl.ds(pl.multiple_of(n * 512, 512), 512)
            out[:, at] = lax.dot_general(
                picks[...], vals[:, at], (((0,), (0,)), ((), ())), preferred_element_type=F32
            )
            return carry

        lax.fori_loop(0, 4, product, 0)

    return kernel


def lookup(values, index):
    return jnp.take_along_axis(values, index, axis=1, mode="promise_in_bounds")


def encode_kernel(pos, p0, p1, p2, p3, enc, bias, dec_bias, sidp, out, cent, pre):
    lane128 = lax.broadcasted_iota(I32, (64, 128), 1)
    for s, part in enumerate((p0, p1, p2, p3)):
        at = pl.ds(pl.multiple_of(lax.rem(pos[0] - s + 4, 4) * 512, 512), 512)
        cent[:, at] = (part[...].astype(F32) - dec_bias[:, at]).astype(BF)

    def product(n, carry):
        cols = pl.ds(pl.multiple_of(n * 256, 256), 256)
        pre[:, cols] = mm(cent[...], enc[:, cols]) + bias[:, cols]
        return carry

    lax.fori_loop(0, 4, product, 0)

    def compress(t, carry):
        rows = pl.ds(pl.multiple_of(t * 64, 64), 64)
        rows_hi = pl.ds(pl.multiple_of(ROWS // 2 + t * 64, 64), 64)
        ids = sidp[rows, :]
        lane = ids & 127
        block = (ids >> 7) - (pos[4] >> 7)
        acc = jnp.zeros((64, 128), F32)
        for b in range(8):
            lo = lookup(pre[rows, b * 128:(b + 1) * 128], lane)
            hi = lookup(pre[rows_hi, b * 128:(b + 1) * 128], lane)
            acc = jnp.where(block == b, jnp.where(lane128 < 64, lo, hi), acc)
        out[rows, :] = acc
        return carry

    lax.fori_loop(0, ROWS // 128, compress, 0)


def decode_kernel(pos, total, table, dec, *refs):
    outs, act, dense, y = refs[:4], refs[4], refs[5], refs[6]
    act[...] = jnp.maximum(total[...], 0.0)

    def step(t, carry):
        rows = pl.ds(pl.multiple_of(t * 64, 64), 64)
        vals = act[pl.ds(pl.multiple_of(lax.rem(t, ROWS // 128) * 64, 64), 64), :]
        for b in range(8):
            idx = table[rows, b * 128:(b + 1) * 128].astype(I32)
            got = lookup(vals, jnp.maximum(idx, 0))
            dense[rows, b * 128:(b + 1) * 128] = jnp.where(idx >= 0, got, 0.0).astype(BF)
        return carry

    lax.fori_loop(0, ROWS // 64, step, 0)

    def product(g, carry):
        at = pl.ds(pl.multiple_of(g * 256, 256), 256)
        y[:, at] = mm(dense[...], dec[:, at]).astype(BF)
        return carry

    lax.fori_loop(0, 8, product, 0)
    for s in range(4):
        first = pl.multiple_of(lax.rem(pos[0] + s, 4) * SEATS, SEATS)
        outs[s][...] = y[pl.ds(first, SEATS), :]


def swap(x, axis):
    return lax.ppermute(x, axis, [(0, 1), (1, 0)])


def dp_shift(x, s):
    return lax.ppermute(x, "dp", [(i, (i + s) % 4) for i in range(4)])


def body(resid, norm_gain, gate_w, up_w, down_w, enc, enc_bias, dec, dec_bias, ids):
    d, x, c = lax.axis_index("dp"), lax.axis_index("xlo"), lax.axis_index("core")
    h, z = lax.axis_index("xhi"), lax.axis_index("z")
    tensor = h * 8 + z
    pos = jnp.stack([d, x, c, tensor, (d * 16 + tensor) * 1024, d, d, d]).astype(I32)

    wide = norm_gain.reshape(1, 2048)
    mine, give = call(split_kernel, [sds((64, 2048), BF)] * 2, 1, [], 0, 1_000_000)(pos, resid)
    other, gain_o = swap(give, "core"), swap(wide, "core")
    gate, up, down = gate_w[0], up_w[0], down_w[:, 0, :]
    gate_o, up_o, down_o = swap(gate, "core"), swap(up, "core"), swap(down, "core")
    *xw, gain = call(
        width_kernel, [sds((64, 1024), BF)] * 4 + [sds((1, 1024), F32)], 4, [], 0, 1_000_000
    )(pos, mine, other, wide, gain_o)
    xs = [xw[0]] + [dp_shift(xw[s], s) for s in range(1, 4)]

    rank = jnp.sum((ids[:, :, None] < ids[:, None, :]).astype(I32), axis=1)
    place = lax.broadcasted_iota(I32, (1, 64, 64), 1)
    sid = jnp.sum(jnp.where(rank[:, None, :] == place, ids[:, None, :], 0), axis=2)
    id_hi, id_lo = ((sid + 1) >> 8).astype(BF), ((sid + 1) & 255).astype(BF)
    slabs = ids >> 10
    uses = jnp.stack([jnp.any(slabs == a * 16 + tensor, axis=1) for a in range(4)]).reshape(16, 128)
    before = (lax.broadcasted_iota(I32, (128, 128), 0) < lax.broadcasted_iota(I32, (128, 128), 1)).astype(BF)
    rank = jnp.where(uses, mm(uses.astype(BF), before).astype(I32), -1)
    every = lax.broadcasted_iota(I32, (1, 1, 64), 2)
    used = jnp.any(slabs[:, :, None] == every, axis=1)
    fullest = jnp.max(jnp.sum(used.reshape(4, 128, 64).astype(I32), axis=1))

    res = call(
        gate_kernel, [sds((64, 1024), BF)] * 4 + [sds((16, 1024), F32), sds((256, 1024), BF)], 7,
        [pltpu.VMEM((256, 1024), BF), pltpu.VMEM((256, 1024), F32)], 470_000_000, 3_000_000,
    )(pos, *xs, gain, gate, gate_o)
    xsel, xg = res[4], res[5]
    res_u = call(
        up_kernel, [sds((64, 896), BF)] * 4, 3, [pltpu.VMEM((256, 896), BF)], 470_000_000, 3_000_000
    )(pos, xg, up, up_o)

    def width_sum(pieces):
        tot = pieces[0].astype(F32)
        for s in range(1, 4):
            tot = tot + dp_shift(pieces[s], s).astype(F32)
        return tot + swap(tot.astype(BF), "xlo").astype(F32)

    tot_g, tot_u = width_sum(res[:4]), width_sum(res_u)
    inv = lax.rsqrt((tot_g[:, 896:897] + tot_g[:, 897:898]) / 8192 + 1e-05)
    hidden = (jax.nn.silu(tot_g[:, :896] * inv) * (tot_u * inv)).astype(BF)
    hid = [hidden] + [dp_shift(hidden, s) for s in range(1, 4)]
    terms = call(
        down_kernel, sds((256, 1024), BF), 6, [pltpu.VMEM((256, 896), BF)], 470_000_000, 3_000_000
    )(pos, *hid, down, down_o)
    terms = lax.all_to_all(terms, ("xhi", "z"), 0, 0, tiled=True)
    block_sum = jnp.sum(terms.reshape(16, 16, 1024).astype(F32), axis=0)
    rows = (xsel + block_sum).astype(BF)

    own, crossed = rows[:, :512], swap(rows[:, 512:], "core")
    rows = jnp.where(c == 0, jnp.stack([own, crossed]), jnp.stack([crossed, own])).reshape(32, 512)
    rows = jnp.broadcast_to(rows[None], (16, 32, 512)).reshape(512, 512)
    rows = lax.all_to_all(rows, ("xhi", "z"), 0, 0, tiled=True)

    lead = ((x == 0) & (c == 0)).astype(F32)
    bias = (enc_bias * lead).reshape(1, 1024)
    wide_bias = dec_bias.reshape(1, 2048)

    def sparse_round(start):
        packed = call(
            pack_kernel(start), [sds((ROWS, 512), BF)] * 4, 2, [], 300_000_000, 2_000_000
        )(pos, rows, rank)
        parts = [packed[0]] + [dp_shift(packed[s], s) for s in range(1, 4)]
        at, _ = lax.optimization_barrier((pos, packed[3]))
        seated = call(ids_kernel(start), sds((ROWS, 64), I32), 3, [], 10_000_000, 200_000)(
            at, id_hi, id_lo, rank
        )
        table = call(table_kernel, sds((ROWS, 1024), jnp.int8), 1, [], 500_000_000, 10_000_000)(at, seated)
        paired = jnp.concatenate([seated[:ROWS // 2], seated[ROWS // 2:]], axis=1)
        paired, table = lax.optimization_barrier((paired, table))
        comp = call(
            encode_kernel, sds((ROWS // 2, 128), F32), 8,
            [pltpu.VMEM((ROWS, 2048), BF), pltpu.VMEM((ROWS, 1024), F32)],
            1_100_000_000, 6_000_000, limit=20,
        )(pos, *parts, enc, bias, wide_bias, paired)
        for axis in ("core", "xlo"):
            comp = comp + swap(comp.astype(BF), axis).astype(F32)
        ys = call(
            decode_kernel, [sds((SEATS, 2048), BF)] * 4, 3,
            [pltpu.VMEM((ROWS // 2, 128), F32), pltpu.VMEM((ROWS, 1024), BF), pltpu.VMEM((ROWS, 2048), BF)],
            1_100_000_000, 8_000_000, limit=20,
        )(pos, comp, table, dec)
        ys = [ys[0]] + [dp_shift(ys[s], s) for s in range(1, 4)]
        return call(
            unpack_kernel(start), sds((128, 2048), F32), 5,
            [pltpu.VMEM((ROWS, 128), BF), pltpu.VMEM((ROWS, 2048), BF)], 140_000_000, 2_000_000,
        )(pos, *ys, rank)

    y = sparse_round(0)
    y = lax.cond(fullest > SEATS, lambda v: v + sparse_round(SEATS), lambda v: v, y)
    y = lax.all_to_all(y.astype(BF), ("xhi", "z"), 0, 0, tiled=True)
    decoded = jnp.sum(y.reshape(16, 8, 2048).astype(F32), axis=0) + wide_bias

    rel = jnp.stack(
        [
            (lambda v: dp_shift(v, s) if s else v)(
                lax.dynamic_slice_in_dim(rows, lax.rem(d + s, 4) * 128 + tensor * 8, 8, 0)
            )
            for s in range(4)
        ]
    )
    kept = jnp.concatenate(
        [lax.dynamic_index_in_dim(rel, (d - g + 4) % 4, 0, keepdims=False) for g in range(4)], 1
    )
    kept_f = kept.astype(F32)
    misfit = kept_f - decoded
    sums = jnp.stack([jnp.sum(misfit * misfit, axis=1), jnp.sum(kept_f * kept_f, axis=1)])
    for axis in ("core", "xlo"):
        sums = sums + swap(sums, axis)
    return kept, decoded.astype(BF), sums[0] / (sums[1] + 1e-06)


def solution(mesh):
    fine = Mesh(mesh.devices.reshape(4, 2, 8, 2, 2), ("dp", "xhi", "z", "xlo", "core"))
    rep, tensor, slabs = ("xlo", "core"), ("xhi", "z"), ("dp", "xhi", "z")
    in_specs = (
        P("dp", rep), P(rep), P(rep, "dp", tensor), P(rep, "dp", tensor), P(tensor, rep, "dp"),
        P(rep, slabs), P(slabs), P(slabs, rep), P(rep), P(),
    )
    out_specs = (P(slabs, rep), P(slabs, rep), P(slabs))
    return jax.shard_map(body, mesh=fine, in_specs=in_specs, out_specs=out_specs, check_vma=False)
```

```python
import jax
import jax.numpy as jnp
from jax import lax
from jax.experimental import pallas as pl
from jax.experimental.pallas import tpu as pltpu
from jax.sharding import Mesh, PartitionSpec as P

BF = jnp.bfloat16
F32 = jnp.float32
I32 = jnp.int32
VM = pl.BlockSpec(memory_space=pltpu.VMEM)
SM = pl.BlockSpec(memory_space=pltpu.SMEM)
ANY = pl.BlockSpec(memory_space=pltpu.HBM)
MIB = 1 << 20


def call(kernel, outs, n_in, scratch, flops, nbytes, limit=12, any_at=(), any_out=False):
    in_specs = [SM] + [ANY if i in any_at else VM for i in range(n_in)]
    return pl.pallas_call(
        kernel,
        out_shape=outs,
        in_specs=in_specs,
        out_specs=jax.tree.map(lambda _: ANY if any_out else VM, outs),
        scratch_shapes=scratch,
        compiler_params=pltpu.CompilerParams(vmem_limit_bytes=limit * MIB),
        cost_estimate=pl.CostEstimate(flops=flops, bytes_accessed=nbytes, transcendentals=0),
    )


def sds(shape, dt):
    return jax.ShapeDtypeStruct(shape, dt)


def mm(a, b):
    return jnp.dot(a, b, preferred_element_type=F32)


SEATS = 64
ROWS = 4 * SEATS


def gate_kernel(pos, p0, p1, p2, p3, gain, go, gp, *refs):
    outs, xsel, xg, pk, xr = refs[:4], refs[4], refs[5], refs[6], refs[7]
    for s, part in enumerate((p0, p1, p2, p3)):
        xr[s * 64:(s + 1) * 64, :] = part[...].astype(F32)
    xf = xr[...]
    xg[...] = (xf * gain[...]).astype(BF)
    ss = jnp.sum(xf * xf, axis=1, keepdims=True)
    hi = ss.astype(BF)
    lo = (ss - hi.astype(F32)).astype(BF)
    lane = lax.broadcasted_iota(I32, (256, 128), 1)
    tail = jnp.where(lane == 0, hi.astype(F32), jnp.where(lane == 1, lo.astype(F32), 0.0))
    pk[:, 896:] = tail.astype(BF)
    pk[:, :896] = (mm(xg[:, :512], go[...]) + mm(xg[:, 512:], gp[...])).astype(BF)
    for s in range(4):
        first = ((4 - s) % 4) * 64
        outs[s][...] = pk[first:first + 64, :]
    group = pos[3] // 4
    first = pl.multiple_of(lax.rem(pos[0] - group + 4, 4) * 64 + lax.rem(pos[3], 4) * 16, 16)
    xsel[...] = xr[pl.ds(first, 16), :]


def up_kernel(pos, xg, uo, up, *refs):
    outs, pk = refs[:4], refs[4]
    pk[...] = (mm(xg[:, :512], uo[...]) + mm(xg[:, 512:], up[...])).astype(BF)
    for s in range(4):
        first = ((4 - s) % 4) * 64
        outs[s][...] = pk[first:first + 64, :]


def down_kernel(pos, *refs):
    parts, down_own, down_oth, out, hid = refs[:4], refs[4], refs[5], refs[6], refs[7]
    for s in range(4):
        first = pl.multiple_of(lax.rem(pos[0] - s + 4, 4) * 64, 64)
        hid[pl.ds(first, 64), :] = parts[s][...]
    for q, w in enumerate((down_own, down_oth)):
        out[:, q * 512:(q + 1) * 512] = mm(hid[...], w[...]).astype(BF)


def split_kernel(pos, resid, mine, give):
    c = pos[2]
    for b in range(4):
        mine[b * 16:(b + 1) * 16, :] = resid[pl.ds(pl.multiple_of(b * 32 + c * 16, 16), 16), :]
        give[b * 16:(b + 1) * 16, :] = resid[pl.ds(pl.multiple_of(b * 32 + (1 - c) * 16, 16), 16), :]


def width_kernel(pos, mine, other, gain, gain_o, *outs):
    for s in range(4):
        col = pl.multiple_of(lax.rem(pos[0] + s, 4) * 512, 512)
        outs[s][:, :512] = mine[:, pl.ds(col, 512)]
        outs[s][:, 512:] = other[:, pl.ds(col, 512)]
    col = pl.multiple_of(pos[0] * 512, 512)
    outs[4][:, :512] = gain[:, pl.ds(col, 512)]
    outs[4][:, 512:] = gain_o[:, pl.ds(col, 512)]


def table_kernel(pos, sid, out):
    lane128 = lax.broadcasted_iota(I32, (32, 128), 1)
    block0 = pos[4] >> 7

    def step(t, carry):
        rows = pl.ds(pl.multiple_of(t * 32, 32), 32)
        ids = sid[rows, :]
        base = jnp.where(t >= ROWS // 64, 64, 0)
        slots = []
        for s in range(8):
            acc = jnp.full((32, 128), -1, I32)
            for i in range(8):
                j = s * 8 + i
                acc = jnp.where((ids[:, j:j + 1] & 127) == lane128, base + j, acc)
            slots.append((jnp.broadcast_to((ids[:, s * 8:s * 8 + 1] >> 7) - block0, (32, 128)), acc))
        for b in range(8):
            acc = jnp.full((32, 128), -1, I32)
            for block, slot in slots:
                acc = jnp.where(block == b, slot, acc)
            out[rows, b * 128:(b + 1) * 128] = acc.astype(jnp.int8)
        return carry

    lax.fori_loop(0, ROWS // 32, step, 0)


def chosen(rank, row, start):
    seat = lax.broadcasted_iota(I32, (SEATS, 128), 0)
    return jnp.where(rank[pl.ds(row, 1), :] == seat + start, 1.0, 0.0).astype(BF)


def pack_kernel():
    def kernel(pos, rows, rank, *outs):
        for s in range(4):
            slab = lax.rem(pos[0] + s, 4)
            for g in range(4):
                pick = chosen(rank, slab * 4 + g, pos[5])
                outs[s][g * SEATS:(g + 1) * SEATS, :] = mm(pick, rows[g * 128:(g + 1) * 128, :]).astype(BF)

    return kernel


def ids_kernel():
    def kernel(pos, hi, lo, rank, out):
        for g in range(4):
            pick = chosen(rank, pos[0] * 4 + g, pos[5])
            at = slice(g * 128, (g + 1) * 128)
            both = mm(pick, hi[at, :]) * 256.0 + mm(pick, lo[at, :])
            out[g * SEATS:(g + 1) * SEATS, :] = both.astype(I32) - 1

    return kernel


def unpack_kernel():
    def kernel(pos, p0, p1, p2, p3, rank, out, picks, vals):
        for s, part in enumerate((p0, p1, p2, p3)):
            slab = lax.rem(pos[0] - s + 4, 4)
            picks[s * SEATS:(s + 1) * SEATS, :] = chosen(rank, slab * 4 + pos[0], pos[5])
            vals[s * SEATS:(s + 1) * SEATS, :] = part[...]

        def product(n, carry):
            at = pl.ds(pl.multiple_of(n * 512, 512), 512)
            out[:, at] = lax.dot_general(
                picks[...], vals[:, at], (((0,), (0,)), ((), ())), preferred_element_type=F32
            )
            return carry

        lax.fori_loop(0, 4, product, 0)

    return kernel


def lookup(values, index):
    return jnp.take_along_axis(values, index, axis=1, mode="promise_in_bounds")


def encode_kernel(pos, p0, p1, p2, p3, enc, bias, dec_bias, sidp, out, cent, pre):
    lane128 = lax.broadcasted_iota(I32, (64, 128), 1)
    for s, part in enumerate((p0, p1, p2, p3)):
        at = pl.ds(pl.multiple_of(lax.rem(pos[0] - s + 4, 4) * 512, 512), 512)
        cent[:, at] = (part[...].astype(F32) - dec_bias[:, at]).astype(BF)

    def product(n, carry):
        cols = pl.ds(pl.multiple_of(n * 256, 256), 256)
        pre[:, cols] = mm(cent[...], enc[:, cols]) + bias[:, cols]
        return carry

    lax.fori_loop(0, 4, product, 0)

    def compress(t, carry):
        rows = pl.ds(pl.multiple_of(t * 64, 64), 64)
        rows_hi = pl.ds(pl.multiple_of(ROWS // 2 + t * 64, 64), 64)
        ids = sidp[rows, :]
        lane = ids & 127
        block = (ids >> 7) - (pos[4] >> 7)
        acc = jnp.zeros((64, 128), F32)
        for b in range(8):
            lo = lookup(pre[rows, b * 128:(b + 1) * 128], lane)
            hi = lookup(pre[rows_hi, b * 128:(b + 1) * 128], lane)
            acc = jnp.where(block == b, jnp.where(lane128 < 64, lo, hi), acc)
        out[rows, :] = acc
        return carry

    lax.fori_loop(0, ROWS // 128, compress, 0)


def decode_kernel(pos, total, table, dec, *refs):
    outs, act, dense, y = refs[:4], refs[4], refs[5], refs[6]
    act[...] = jnp.maximum(total[...], 0.0)

    def step(t, carry):
        rows = pl.ds(pl.multiple_of(t * 64, 64), 64)
        vals = act[pl.ds(pl.multiple_of(lax.rem(t, ROWS // 128) * 64, 64), 64), :]
        for b in range(8):
            idx = table[rows, b * 128:(b + 1) * 128].astype(I32)
            got = lookup(vals, jnp.maximum(idx, 0))
            dense[rows, b * 128:(b + 1) * 128] = jnp.where(idx >= 0, got, 0.0).astype(BF)
        return carry

    lax.fori_loop(0, ROWS // 64, step, 0)

    def product(g, carry):
        at = pl.ds(pl.multiple_of(g * 256, 256), 256)
        y[:, at] = mm(dense[...], dec[:, at]).astype(BF)
        return carry

    lax.fori_loop(0, 8, product, 0)
    for s in range(4):
        first = pl.multiple_of(lax.rem(pos[0] + s, 4) * SEATS, SEATS)
        outs[s][...] = y[pl.ds(first, SEATS), :]


def swap(x, axis):
    return lax.ppermute(x, axis, [(0, 1), (1, 0)])


def dp_shift(x, s):
    return lax.ppermute(x, "dp", [(i, (i + s) % 4) for i in range(4)])


def body(resid, norm_gain, gate_w, up_w, down_w, enc, enc_bias, dec, dec_bias, ids):
    d, x, c = lax.axis_index("dp"), lax.axis_index("xlo"), lax.axis_index("core")
    h, z = lax.axis_index("xhi"), lax.axis_index("z")
    tensor = h * 8 + z
    pos = jnp.stack([d, x, c, tensor, (d * 16 + tensor) * 1024, d, d, d]).astype(I32)

    wide = norm_gain.reshape(1, 2048)
    mine, give = call(split_kernel, [sds((64, 2048), BF)] * 2, 1, [], 0, 1_000_000)(pos, resid)
    other, gain_o = swap(give, "core"), swap(wide, "core")
    gate, up, down = gate_w[0], up_w[0], down_w[:, 0, :]
    gate_o, up_o, down_o = swap(gate, "core"), swap(up, "core"), swap(down, "core")
    *xw, gain = call(
        width_kernel, [sds((64, 1024), BF)] * 4 + [sds((1, 1024), F32)], 4, [], 0, 1_000_000
    )(pos, mine, other, wide, gain_o)
    xs = [xw[0]] + [dp_shift(xw[s], s) for s in range(1, 4)]

    rank = jnp.sum((ids[:, :, None] < ids[:, None, :]).astype(I32), axis=1)
    place = lax.broadcasted_iota(I32, (1, 64, 64), 1)
    sid = jnp.sum(jnp.where(rank[:, None, :] == place, ids[:, None, :], 0), axis=2)
    id_hi, id_lo = ((sid + 1) >> 8).astype(BF), ((sid + 1) & 255).astype(BF)
    slabs = ids >> 10
    uses = jnp.stack([jnp.any(slabs == a * 16 + tensor, axis=1) for a in range(4)]).reshape(16, 128)
    before = (lax.broadcasted_iota(I32, (128, 128), 0) < lax.broadcasted_iota(I32, (128, 128), 1)).astype(BF)
    rank = jnp.where(uses, mm(uses.astype(BF), before).astype(I32), -1)
    res = call(
        gate_kernel, [sds((64, 1024), BF)] * 4 + [sds((16, 1024), F32), sds((256, 1024), BF)], 7,
        [pltpu.VMEM((256, 1024), BF), pltpu.VMEM((256, 1024), F32)], 470_000_000, 3_000_000,
    )(pos, *xs, gain, gate, gate_o)
    xsel, xg = res[4], res[5]
    res_u = call(
        up_kernel, [sds((64, 896), BF)] * 4, 3, [pltpu.VMEM((256, 896), BF)], 470_000_000, 3_000_000
    )(pos, xg, up, up_o)

    def width_sum(pieces):
        tot = pieces[0].astype(F32)
        for s in range(1, 4):
            tot = tot + dp_shift(pieces[s], s).astype(F32)
        return tot + swap(tot.astype(BF), "xlo").astype(F32)

    tot_g, tot_u = width_sum(res[:4]), width_sum(res_u)
    inv = lax.rsqrt((tot_g[:, 896:897] + tot_g[:, 897:898]) / 8192 + 1e-05)
    hidden = (jax.nn.silu(tot_g[:, :896] * inv) * (tot_u * inv)).astype(BF)
    hid = [hidden] + [dp_shift(hidden, s) for s in range(1, 4)]
    terms = call(
        down_kernel, sds((256, 1024), BF), 6, [pltpu.VMEM((256, 896), BF)], 470_000_000, 3_000_000
    )(pos, *hid, down, down_o)
    terms = lax.all_to_all(terms, ("xhi", "z"), 0, 0, tiled=True)
    block_sum = jnp.sum(terms.reshape(16, 16, 1024).astype(F32), axis=0)
    rows = (xsel + block_sum).astype(BF)

    own, crossed = rows[:, :512], swap(rows[:, 512:], "core")
    rows = jnp.where(c == 0, jnp.stack([own, crossed]), jnp.stack([crossed, own])).reshape(32, 512)
    rows = jnp.broadcast_to(rows[None], (16, 32, 512)).reshape(512, 512)
    slabs_late, _ = lax.optimization_barrier((slabs, rows))
    every = lax.broadcasted_iota(I32, (1, 1, 64), 2)
    used = jnp.any(slabs_late[:, :, None] == every, axis=1)
    fullest = jnp.max(jnp.sum(used.reshape(4, 128, 64).astype(I32), axis=1))
    rows = lax.all_to_all(rows, ("xhi", "z"), 0, 0, tiled=True)

    lead = ((x == 0) & (c == 0)).astype(F32)
    bias = (enc_bias * lead).reshape(1, 1024)
    wide_bias = dec_bias.reshape(1, 2048)

    def dp_all(pieces):
        return [pieces[0]] + [dp_shift(pieces[s], s) for s in range(1, 4)]

    def sparse_round(start, pos=pos):
        pos = pos.at[5].set(start)
        packed = call(
            pack_kernel(), [sds((ROWS, 512), BF)] * 4, 2, [], 300_000_000, 2_000_000
        )(pos, rows, rank)
        parts = dp_all(packed)
        at, _ = lax.optimization_barrier((pos, packed[3]))
        seated = call(ids_kernel(), sds((ROWS, 64), I32), 3, [], 10_000_000, 200_000)(
            at, id_hi, id_lo, rank
        )
        table = call(table_kernel, sds((ROWS, 1024), jnp.int8), 1, [], 500_000_000, 10_000_000)(at, seated)
        paired = jnp.concatenate([seated[:ROWS // 2], seated[ROWS // 2:]], axis=1)
        paired, table = lax.optimization_barrier((paired, table))
        comp = call(
            encode_kernel, sds((ROWS // 2, 128), F32), 8,
            [pltpu.VMEM((ROWS, 2048), BF), pltpu.VMEM((ROWS, 1024), F32)],
            1_100_000_000, 6_000_000, limit=20,
        )(pos, *parts, enc, bias, wide_bias, paired)
        for axis in ("core", "xlo"):
            comp = comp + swap(comp.astype(BF), axis).astype(F32)
        ys = call(
            decode_kernel, [sds((SEATS, 2048), BF)] * 4, 3,
            [pltpu.VMEM((ROWS // 2, 128), F32), pltpu.VMEM((ROWS, 1024), BF), pltpu.VMEM((ROWS, 2048), BF)],
            1_100_000_000, 8_000_000, limit=20,
        )(pos, comp, table, dec)
        ys = dp_all(ys)
        return call(
            unpack_kernel(), sds((128, 2048), F32), 5,
            [pltpu.VMEM((ROWS, 128), BF), pltpu.VMEM((ROWS, 2048), BF)], 140_000_000, 2_000_000,
        )(pos, *ys, rank)

    rounds = lax.div(fullest + SEATS - 1, SEATS)
    y = lax.fori_loop(0, rounds, lambda i, v: v + sparse_round(i * SEATS), jnp.zeros((128, 2048), F32))
    y = lax.all_to_all(y.astype(BF), ("xhi", "z"), 0, 0, tiled=True)
    decoded = jnp.sum(y.reshape(16, 8, 2048).astype(F32), axis=0) + wide_bias

    rel = jnp.stack(
        dp_all([lax.dynamic_slice_in_dim(rows, lax.rem(d + s, 4) * 128 + tensor * 8, 8, 0) for s in range(4)])
    )
    kept = jnp.concatenate(
        [lax.dynamic_index_in_dim(rel, (d - g + 4) % 4, 0, keepdims=False) for g in range(4)], 1
    )
    kept_f = kept.astype(F32)
    misfit = kept_f - decoded
    sums = jnp.stack([jnp.sum(misfit * misfit, axis=1), jnp.sum(kept_f * kept_f, axis=1)])
    for axis in ("core", "xlo"):
        sums = sums + swap(sums, axis)
    return kept, decoded.astype(BF), sums[0] / (sums[1] + 1e-06)


def solution(mesh):
    fine = Mesh(mesh.devices.reshape(4, 2, 8, 2, 2), ("dp", "xhi", "z", "xlo", "core"))
    rep, tensor, slabs = ("xlo", "core"), ("xhi", "z"), ("dp", "xhi", "z")
    in_specs = (
        P("dp", rep), P(rep), P(rep, "dp", tensor), P(rep, "dp", tensor), P(tensor, rep, "dp"),
        P(rep, slabs), P(slabs), P(slabs, rep), P(rep), P(),
    )
    out_specs = (P(slabs, rep), P(slabs, rep), P(slabs))
    return jax.shard_map(body, mesh=fine, in_specs=in_specs, out_specs=out_specs, check_vma=False)
```

```python
import jax
import jax.numpy as jnp
from jax import lax
from jax.experimental import pallas as pl
from jax.experimental.pallas import tpu as pltpu
from jax.sharding import Mesh, PartitionSpec as P

BF = jnp.bfloat16
F32 = jnp.float32
I32 = jnp.int32
VM = pl.BlockSpec(memory_space=pltpu.VMEM)
SM = pl.BlockSpec(memory_space=pltpu.SMEM)
ANY = pl.BlockSpec(memory_space=pltpu.HBM)
MIB = 1 << 20


def call(kernel, outs, n_in, scratch, flops, nbytes, limit=12, any_at=(), any_out=False):
    in_specs = [SM] + [ANY if i in any_at else VM for i in range(n_in)]
    return pl.pallas_call(
        kernel,
        out_shape=outs,
        in_specs=in_specs,
        out_specs=jax.tree.map(lambda _: ANY if any_out else VM, outs),
        scratch_shapes=scratch,
        compiler_params=pltpu.CompilerParams(vmem_limit_bytes=limit * MIB),
        cost_estimate=pl.CostEstimate(flops=flops, bytes_accessed=nbytes, transcendentals=0),
    )


def sds(shape, dt):
    return jax.ShapeDtypeStruct(shape, dt)


def mm(a, b):
    return jnp.dot(a, b, preferred_element_type=F32)


SEATS = 64
ROWS = 4 * SEATS


def gate_kernel(pos, p0, p1, p2, p3, gain, go, gp, *refs):
    outs, xsel, xg, pk, xr = refs[:4], refs[4], refs[5], refs[6], refs[7]
    for s, part in enumerate((p0, p1, p2, p3)):
        xr[s * 64:(s + 1) * 64, :] = part[...].astype(F32)
    xf = xr[...]
    xg[...] = (xf * gain[...]).astype(BF)
    ss = jnp.sum(xf * xf, axis=1, keepdims=True)
    hi = ss.astype(BF)
    lo = (ss - hi.astype(F32)).astype(BF)
    lane = lax.broadcasted_iota(I32, (256, 128), 1)
    tail = jnp.where(lane == 0, hi.astype(F32), jnp.where(lane == 1, lo.astype(F32), 0.0))
    pk[:, 896:] = tail.astype(BF)
    pk[:, :896] = (mm(xg[:, :512], go[...]) + mm(xg[:, 512:], gp[...])).astype(BF)
    for s in range(4):
        first = ((4 - s) % 4) * 64
        outs[s][...] = pk[first:first + 64, :]
    group = pos[3] // 4
    first = pl.multiple_of(lax.rem(pos[0] - group + 4, 4) * 64 + lax.rem(pos[3], 4) * 16, 16)
    xsel[...] = xr[pl.ds(first, 16), :]


def up_kernel(pos, xg, uo, up, *refs):
    outs, pk = refs[:4], refs[4]
    pk[...] = (mm(xg[:, :512], uo[...]) + mm(xg[:, 512:], up[...])).astype(BF)
    for s in range(4):
        first = ((4 - s) % 4) * 64
        outs[s][...] = pk[first:first + 64, :]


def down_kernel(pos, *refs):
    parts, down_own, down_oth, out, hid = refs[:4], refs[4], refs[5], refs[6], refs[7]
    for s in range(4):
        first = pl.multiple_of(lax.rem(pos[0] - s + 4, 4) * 64, 64)
        hid[pl.ds(first, 64), :] = parts[s][...]
    for q, w in enumerate((down_own, down_oth)):
        out[:, q * 512:(q + 1) * 512] = mm(hid[...], w[...]).astype(BF)


def split_kernel(pos, resid, mine, give):
    c = pos[2]
    for b in range(4):
        mine[b * 16:(b + 1) * 16, :] = resid[pl.ds(pl.multiple_of(b * 32 + c * 16, 16), 16), :]
        give[b * 16:(b + 1) * 16, :] = resid[pl.ds(pl.multiple_of(b * 32 + (1 - c) * 16, 16), 16), :]


def width_kernel(pos, mine, other, gain, gain_o, *outs):
    for s in range(4):
        col = pl.multiple_of(lax.rem(pos[0] + s, 4) * 512, 512)
        outs[s][:, :512] = mine[:, pl.ds(col, 512)]
        outs[s][:, 512:] = other[:, pl.ds(col, 512)]
    col = pl.multiple_of(pos[0] * 512, 512)
    outs[4][:, :512] = gain[:, pl.ds(col, 512)]
    outs[4][:, 512:] = gain_o[:, pl.ds(col, 512)]


def table_kernel(pos, sid, out):
    lane128 = lax.broadcasted_iota(I32, (32, 128), 1)
    block0 = pos[4] >> 7

    def step(t, carry):
        rows = pl.ds(pl.multiple_of(t * 32, 32), 32)
        ids = sid[rows, :]
        base = jnp.where(t >= ROWS // 64, 64, 0)
        slots = []
        for s in range(8):
            acc = jnp.full((32, 128), -1, I32)
            for i in range(8):
                j = s * 8 + i
                acc = jnp.where((ids[:, j:j + 1] & 127) == lane128, base + j, acc)
            slots.append((jnp.broadcast_to((ids[:, s * 8:s * 8 + 1] >> 7) - block0, (32, 128)), acc))
        for b in range(8):
            acc = jnp.full((32, 128), -1, I32)
            for block, slot in slots:
                acc = jnp.where(block == b, slot, acc)
            out[rows, b * 128:(b + 1) * 128] = acc.astype(jnp.int8)
        return carry

    lax.fori_loop(0, ROWS // 32, step, 0)


def chosen(rank, row, start):
    seat = lax.broadcasted_iota(I32, (SEATS, 128), 0)
    return jnp.where(rank[pl.ds(row, 1), :] == seat + start, 1.0, 0.0).astype(BF)


def pack_kernel():
    def kernel(pos, rows, rank, *outs):
        for s in range(4):
            slab = lax.rem(pos[0] + s, 4)
            for g in range(4):
                pick = chosen(rank, slab * 4 + g, pos[5])
                outs[s][g * SEATS:(g + 1) * SEATS, :] = mm(pick, rows[g * 128:(g + 1) * 128, :]).astype(BF)

    return kernel


def ids_kernel():
    def kernel(pos, hi, lo, rank, out):
        for g in range(4):
            pick = chosen(rank, pos[0] * 4 + g, pos[5])
            at = slice(g * 128, (g + 1) * 128)
            both = mm(pick, hi[at, :]) * 256.0 + mm(pick, lo[at, :])
            out[g * SEATS:(g + 1) * SEATS, :] = both.astype(I32) - 1

    return kernel


def unpack_kernel():
    def kernel(pos, p0, p1, p2, p3, rank, out, picks, vals):
        for s, part in enumerate((p0, p1, p2, p3)):
            slab = lax.rem(pos[0] - s + 4, 4)
            picks[s * SEATS:(s + 1) * SEATS, :] = chosen(rank, slab * 4 + pos[0], pos[5])
            vals[s * SEATS:(s + 1) * SEATS, :] = part[...]

        def product(n, carry):
            at = pl.ds(pl.multiple_of(n * 512, 512), 512)
            out[:, at] = lax.dot_general(
                picks[...], vals[:, at], (((0,), (0,)), ((), ())), preferred_element_type=F32
            )
            return carry

        lax.fori_loop(0, 4, product, 0)

    return kernel


def lookup(values, index):
    return jnp.take_along_axis(values, index, axis=1, mode="promise_in_bounds")


def encode_kernel(pos, p0, p1, p2, p3, enc, bias, dec_bias, sidp, out, cent, pre):
    lane128 = lax.broadcasted_iota(I32, (64, 128), 1)
    for s, part in enumerate((p0, p1, p2, p3)):
        at = pl.ds(pl.multiple_of(lax.rem(pos[0] - s + 4, 4) * 512, 512), 512)
        cent[:, at] = (part[...].astype(F32) - dec_bias[:, at]).astype(BF)

    def product(n, carry):
        cols = pl.ds(pl.multiple_of(n * 256, 256), 256)
        pre[:, cols] = mm(cent[...], enc[:, cols]) + bias[:, cols]
        return carry

    lax.fori_loop(0, 4, product, 0)

    def compress(t, carry):
        rows = pl.ds(pl.multiple_of(t * 64, 64), 64)
        rows_hi = pl.ds(pl.multiple_of(ROWS // 2 + t * 64, 64), 64)
        ids = sidp[rows, :]
        lane = ids & 127
        block = (ids >> 7) - (pos[4] >> 7)
        acc = jnp.zeros((64, 128), F32)
        for b in range(8):
            lo = lookup(pre[rows, b * 128:(b + 1) * 128], lane)
            hi = lookup(pre[rows_hi, b * 128:(b + 1) * 128], lane)
            acc = jnp.where(block == b, jnp.where(lane128 < 64, lo, hi), acc)
        out[rows, :] = acc
        return carry

    lax.fori_loop(0, ROWS // 128, compress, 0)


def decode_kernel(pos, total, table, dec, *refs):
    outs, act, dense, y = refs[:4], refs[4], refs[5], refs[6]
    act[...] = jnp.maximum(total[...], 0.0)

    def step(t, carry):
        rows = pl.ds(pl.multiple_of(t * 64, 64), 64)
        vals = act[pl.ds(pl.multiple_of(lax.rem(t, ROWS // 128) * 64, 64), 64), :]
        for b in range(8):
            idx = table[rows, b * 128:(b + 1) * 128].astype(I32)
            got = lookup(vals, jnp.maximum(idx, 0))
            dense[rows, b * 128:(b + 1) * 128] = jnp.where(idx >= 0, got, 0.0).astype(BF)
        return carry

    lax.fori_loop(0, ROWS // 64, step, 0)

    def product(g, carry):
        at = pl.ds(pl.multiple_of(g * 256, 256), 256)
        y[:, at] = mm(dense[...], dec[:, at]).astype(BF)
        return carry

    lax.fori_loop(0, 8, product, 0)
    for s in range(4):
        first = pl.multiple_of(lax.rem(pos[0] + s, 4) * SEATS, SEATS)
        outs[s][...] = y[pl.ds(first, SEATS), :]


def swap(x, axis):
    return lax.ppermute(x, axis, [(0, 1), (1, 0)])


def dp_shift(x, s):
    return lax.ppermute(x, "dp", [(i, (i + s) % 4) for i in range(4)])


def body(resid, norm_gain, gate_w, up_w, down_w, enc, enc_bias, dec, dec_bias, ids):
    d, x, c = lax.axis_index("dp"), lax.axis_index("xlo"), lax.axis_index("core")
    h, z = lax.axis_index("xhi"), lax.axis_index("z")
    tensor = h * 8 + z
    pos = jnp.stack([d, x, c, tensor, (d * 16 + tensor) * 1024, d, d, d]).astype(I32)

    wide = norm_gain.reshape(1, 2048)
    mine, give = call(split_kernel, [sds((64, 2048), BF)] * 2, 1, [], 0, 1_000_000)(pos, resid)
    other, gain_o = swap(give, "core"), swap(wide, "core")
    gate, up, down = gate_w[0], up_w[0], down_w[:, 0, :]
    gate_o, up_o, down_o = swap(gate, "core"), swap(up, "core"), swap(down, "core")
    *xw, gain = call(
        width_kernel, [sds((64, 1024), BF)] * 4 + [sds((1, 1024), F32)], 4, [], 0, 1_000_000
    )(pos, mine, other, wide, gain_o)
    xs = [xw[0]] + [dp_shift(xw[s], s) for s in range(1, 4)]

    rank = jnp.sum((ids[:, :, None] < ids[:, None, :]).astype(I32), axis=1)
    place = lax.broadcasted_iota(I32, (1, 64, 64), 1)
    sid = jnp.sum(jnp.where(rank[:, None, :] == place, ids[:, None, :], 0), axis=2)
    id_hi, id_lo = ((sid + 1) >> 8).astype(BF), ((sid + 1) & 255).astype(BF)
    slabs = ids >> 10
    uses = jnp.stack([jnp.any(slabs == a * 16 + tensor, axis=1) for a in range(4)]).reshape(16, 128)
    before = (lax.broadcasted_iota(I32, (128, 128), 0) < lax.broadcasted_iota(I32, (128, 128), 1)).astype(BF)
    rank = jnp.where(uses, mm(uses.astype(BF), before).astype(I32), -1)
    res = call(
        gate_kernel, [sds((64, 1024), BF)] * 4 + [sds((16, 1024), F32), sds((256, 1024), BF)], 7,
        [pltpu.VMEM((256, 1024), BF), pltpu.VMEM((256, 1024), F32)], 470_000_000, 3_000_000,
    )(pos, *xs, gain, gate, gate_o)
    xsel, xg = res[4], res[5]
    res_u = call(
        up_kernel, [sds((64, 896), BF)] * 4, 3, [pltpu.VMEM((256, 896), BF)], 470_000_000, 3_000_000
    )(pos, xg, up, up_o)

    def width_sum(pieces):
        tot = pieces[0].astype(F32)
        for s in range(1, 4):
            tot = tot + dp_shift(pieces[s], s).astype(F32)
        return tot + swap(tot.astype(BF), "xlo").astype(F32)

    tot_g, tot_u = width_sum(res[:4]), width_sum(res_u)
    inv = lax.rsqrt((tot_g[:, 896:897] + tot_g[:, 897:898]) / 8192 + 1e-05)
    hidden = (jax.nn.silu(tot_g[:, :896] * inv) * (tot_u * inv)).astype(BF)
    hid = [hidden] + [dp_shift(hidden, s) for s in range(1, 4)]
    terms = call(
        down_kernel, sds((256, 1024), BF), 6, [pltpu.VMEM((256, 896), BF)], 470_000_000, 3_000_000
    )(pos, *hid, down, down_o)
    slabs_late, _ = lax.optimization_barrier((slabs, terms))
    every = lax.broadcasted_iota(I32, (1, 1, 64), 2)
    used = jnp.any(slabs_late[:, :, None] == every, axis=1)
    fullest = jnp.max(jnp.sum(used.reshape(4, 128, 64).astype(I32), axis=1))
    terms = lax.all_to_all(terms, ("xhi", "z"), 0, 0, tiled=True)
    terms, fullest = lax.optimization_barrier((terms, fullest))
    block_sum = jnp.sum(terms.reshape(16, 16, 1024).astype(F32), axis=0)
    rows = (xsel + block_sum).astype(BF)

    own, crossed = rows[:, :512], swap(rows[:, 512:], "core")
    rows = jnp.where(c == 0, jnp.stack([own, crossed]), jnp.stack([crossed, own])).reshape(32, 512)
    rows = jnp.broadcast_to(rows[None], (16, 32, 512)).reshape(512, 512)
    rows = lax.all_to_all(rows, ("xhi", "z"), 0, 0, tiled=True)

    lead = ((x == 0) & (c == 0)).astype(F32)
    bias = (enc_bias * lead).reshape(1, 1024)
    wide_bias = dec_bias.reshape(1, 2048)

    def dp_all(pieces):
        return [pieces[0]] + [dp_shift(pieces[s], s) for s in range(1, 4)]

    def sparse_round(start, pos=pos):
        pos = pos.at[5].set(start)
        packed = call(
            pack_kernel(), [sds((ROWS, 512), BF)] * 4, 2, [], 300_000_000, 2_000_000
        )(pos, rows, rank)
        parts = dp_all(packed)
        at, _ = lax.optimization_barrier((pos, packed[3]))
        seated = call(ids_kernel(), sds((ROWS, 64), I32), 3, [], 10_000_000, 200_000)(
            at, id_hi, id_lo, rank
        )
        table = call(table_kernel, sds((ROWS, 1024), jnp.int8), 1, [], 500_000_000, 10_000_000)(at, seated)
        paired = jnp.concatenate([seated[:ROWS // 2], seated[ROWS // 2:]], axis=1)
        paired, table = lax.optimization_barrier((paired, table))
        comp = call(
            encode_kernel, sds((ROWS // 2, 128), F32), 8,
            [pltpu.VMEM((ROWS, 2048), BF), pltpu.VMEM((ROWS, 1024), F32)],
            1_100_000_000, 6_000_000, limit=20,
        )(pos, *parts, enc, bias, wide_bias, paired)
        for axis in ("core", "xlo"):
            comp = comp + swap(comp.astype(BF), axis).astype(F32)
        ys = call(
            decode_kernel, [sds((SEATS, 2048), BF)] * 4, 3,
            [pltpu.VMEM((ROWS // 2, 128), F32), pltpu.VMEM((ROWS, 1024), BF), pltpu.VMEM((ROWS, 2048), BF)],
            1_100_000_000, 8_000_000, limit=20,
        )(pos, comp, table, dec)
        ys = dp_all(ys)
        return call(
            unpack_kernel(), sds((128, 2048), F32), 5,
            [pltpu.VMEM((ROWS, 128), BF), pltpu.VMEM((ROWS, 2048), BF)], 140_000_000, 2_000_000,
        )(pos, *ys, rank)

    rounds = lax.div(fullest + SEATS - 1, SEATS)
    y = lax.fori_loop(0, rounds, lambda i, v: v + sparse_round(i * SEATS), jnp.zeros((128, 2048), F32))
    y = lax.all_to_all(y.astype(BF), ("xhi", "z"), 0, 0, tiled=True)
    decoded = jnp.sum(y.reshape(16, 8, 2048).astype(F32), axis=0) + wide_bias

    rel = jnp.stack(
        dp_all([lax.dynamic_slice_in_dim(rows, lax.rem(d + s, 4) * 128 + tensor * 8, 8, 0) for s in range(4)])
    )
    kept = jnp.concatenate(
        [lax.dynamic_index_in_dim(rel, (d - g + 4) % 4, 0, keepdims=False) for g in range(4)], 1
    )
    kept_f = kept.astype(F32)
    misfit = kept_f - decoded
    sums = jnp.stack([jnp.sum(misfit * misfit, axis=1), jnp.sum(kept_f * kept_f, axis=1)])
    for axis in ("core", "xlo"):
        sums = sums + swap(sums, axis)
    return kept, decoded.astype(BF), sums[0] / (sums[1] + 1e-06)


def solution(mesh):
    fine = Mesh(mesh.devices.reshape(4, 2, 8, 2, 2), ("dp", "xhi", "z", "xlo", "core"))
    rep, tensor, slabs = ("xlo", "core"), ("xhi", "z"), ("dp", "xhi", "z")
    in_specs = (
        P("dp", rep), P(rep), P(rep, "dp", tensor), P(rep, "dp", tensor), P(tensor, rep, "dp"),
        P(rep, slabs), P(slabs), P(slabs, rep), P(rep), P(),
    )
    out_specs = (P(slabs, rep), P(slabs, rep), P(slabs))
    return jax.shard_map(body, mesh=fine, in_specs=in_specs, out_specs=out_specs, check_vma=False)
```
